256 devices in a mesh: band: 4 (over x_lo, core), fft: 64 (over z, x_hi, y).
Axes of the slice: x: 4 (x_hi: 2, x_lo: 2; x = x_hi * 2 + x_lo), y: 4, z: 8, core: 2. Of those that a mesh axis runs over, the one named last changes fastest.
Arguments:
- orbitals: float32 [4, 128, 128, 128], P('band', 'fft'), may hold values from -6 to 6
- stick_cols: int32 [8192], replicated, may hold values from 0 to 16383, as said below
Outputs:
- exchange_field: float32 [4, 128, 128, 128], P('band', 'fft')
- spectrum: float32 [4, 128, 8192], P('band', None, 'fft')
The draws below stay inside these ranges and needn't reach their ends.
Inputs may be any that keep to these rules, and one draw needn't show every extreme that they name: `stick_cols`: distinct flat column indices kx * 128 + ky; every column with s(kx)^2 + s(ky)^2 <= 48^2 is listed, the other entries are further columns, all in a drawn order.
All inputs are finite; a program needn't handle non-finite values.
Results may differ from the reference program's by a relative error of at most 0.0003.
Values sent between devices are 32-bit elements; how exact they have to be, the bound alone decides.
A program may use at most 64 MiB of HBM per device.

```python
import jax
import jax.numpy as jnp
from jax import lax

N = 128
B_LOC = 1
RAD = 48
NSTICK = 8192
NB = 4
N_BAND = 4


def draw_stick_cols(key, part):
    shuffled = jax.random.permutation(key, jnp.arange(N * N, dtype=jnp.int32))
    row_freq = shuffled // N
    col_freq = shuffled % N
    row_signed = jnp.where(row_freq < N // 2, row_freq, row_freq - N)
    col_signed = jnp.where(col_freq < N // 2, col_freq, col_freq - N)
    outside = (row_signed * row_signed + col_signed * col_signed > RAD * RAD).astype(jnp.int32)
    ranked = jnp.argsort(outside, stable=True)
    return shuffled[ranked][:NSTICK].astype(jnp.int32)


def levels(key, dims, cuts, smallest, largest):
    level = 1.0
    for position, shards_of in cuts:
        steps = jax.random.uniform(jax.random.fold_in(jax.random.fold_in(key, 6), position), (shards_of,), jnp.float32, smallest / len(cuts), largest / len(cuts))
        level = level * jnp.repeat(jnp.exp(steps), dims[position] // shards_of).reshape((-1,) + (1,) * (len(dims) - 1 - position))
    return level


def centred(stream_key, dims, width, reach, split=(), kind=jnp.bfloat16):
    gain = levels(stream_key, dims, split, -0.22, 0.18) if split else 1.0
    values = jax.random.normal(stream_key, dims, jnp.float32) * width * gain
    return jnp.minimum(jnp.maximum(values, -reach), reach).astype(kind)


def setup_inputs(seed: int = 0) -> dict:
    splits = jax.random.split(jax.random.key(seed), 3)
    return {
        "orbitals": centred(splits[0], (NB, N, N, N), 1.0, 6.0, ((0, 4), (1, 64)), jnp.float32),
        "stick_cols": draw_stick_cols(jax.random.fold_in(splits[2], 71), 0),
    }


screening = 16.0
strength = 10.0

def cas_axis(field, axis):
    spectral = jnp.fft.fft(field, axis=axis)
    return (jnp.real(spectral) - jnp.imag(spectral)) / jnp.sqrt(jnp.float32(field.shape[axis]))

def hartley(field):
    for axis in (0, 1, 2):
        field = cas_axis(field, axis)
    return field

def signed(positions):
    return jnp.where(positions < N // 2, positions, positions - N)

def coulomb(squared):
    kappa_float = squared.astype(jnp.float32)
    safe_kappa = jnp.maximum(kappa_float, jnp.float32(1.0))
    values = strength * screening * (1.0 - jnp.exp(-kappa_float / screening)) / safe_kappa
    inside = (squared > 0) & (squared <= RAD * RAD)
    return jnp.where(inside, values, jnp.float32(0.0))

def reference(orbitals, stick_cols):
    freqs = signed(jnp.arange(N, dtype=jnp.int32))
    squares = freqs * freqs
    kernel = coulomb(squares[:, None, None] + squares[None, :, None] + squares[None, None, :])

    def one_band(band_id):
        group = band_id // B_LOC
        own_start = group * B_LOC
        prev_start = (group + N_BAND - 1) % N_BAND * B_LOC
        ramp = jnp.arange(B_LOC, dtype=jnp.int32)
        partner_ids = jnp.concatenate([own_start + ramp, prev_start + ramp]).astype(jnp.int32)
        source = orbitals[band_id]

        def add_pair(carry, partner_id):
            field_sum, energy_sum = carry
            partner = orbitals[partner_id]
            rho_hat = hartley(source * partner)
            pot_hat = kernel * rho_hat
            potential = hartley(pot_hat)
            field_sum = field_sum - potential * partner
            energy = jnp.take((pot_hat * rho_hat).reshape(N, N * N), stick_cols, axis=1)
            return ((field_sum, energy_sum + energy), None)
        start_carry = (jnp.zeros((N, N, N), jnp.float32), jnp.zeros((N, NSTICK), jnp.float32))
        (field_sum, energy_sum), _ = lax.scan(add_pair, start_carry, partner_ids)
        return (field_sum, energy_sum / jnp.float32(2 * B_LOC))
    exchange_field, spectrum = lax.map(one_band, jnp.arange(NB, dtype=jnp.int32))
    return (exchange_field, spectrum)
```

```python
import functools
import math

import jax
import jax.numpy as jnp
import numpy as np
from jax import lax
from jax.experimental import pallas as pl
from jax.experimental.pallas import tpu as pltpu
from jax.sharding import PartitionSpec as P

RAD = 48
N = 128
NF = 64
NBAND = 4
NOWN = 32
PER = 4
STEPS = NOWN // PER
LANES = PER * 2 * N

screening = 16.0
strength = 10.0

MESH = pl.DeviceIdType.MESH
f32 = jnp.float32
bf16 = jnp.bfloat16


def owner_device(o):
    return o


def partner_block(o):
    return o + NOWN


def tables():
    k = np.arange(N)
    angles = 2.0 * math.pi / N * (k[:, None] * k[None, :] % N)
    c = (np.cos(angles) + np.sin(angles)) / math.sqrt(N)
    import ml_dtypes

    hi = c.astype(np.float32).astype(ml_dtypes.bfloat16)
    lo = (c - hi.astype(np.float64)).astype(np.float32).astype(ml_dtypes.bfloat16)
    order = np.concatenate([k[0::2], k[1::2]])
    along_y = np.block([[hi, lo], [hi, lo]])
    split_rows = np.block([[hi[order], hi[order]], [lo[order], lo[order]]])
    split_cols = np.block([[hi[:, order], hi[:, order]], [lo[:, order], lo[:, order]]])
    return along_y, split_rows, split_cols


def two_terms(x):
    hi = x.astype(bf16)
    return hi, (x - hi.astype(f32)).astype(bf16)


def signed(x):
    return jnp.where(x < N // 2, x, x - N)


def coulomb(squared):
    kappa = squared.astype(f32)
    safe = jnp.maximum(kappa, f32(1.0))
    values = strength * screening * (1.0 - jnp.exp(-kappa / screening)) / safe
    inside = (squared > 0) & (squared <= RAD * RAD)
    return jnp.where(inside, values, f32(0.0))


def dot(a, b):
    return jnp.dot(a, b, preferred_element_type=f32)


def left_table(table, x):
    hi, lo = two_terms(x)
    both = dot(table, jnp.concatenate([hi, lo], axis=0))
    return both[:N] + both[N:]


def right_table(x, table):
    hi, lo = two_terms(x)
    both = dot(jnp.concatenate([hi, lo], axis=1), table)
    return both[:, :N] + both[:, N:]


def kernel(
    orb_hbm, cols, taby_hbm, tabf_hbm, tabi_hbm, field, spec,
    own, prev, taby, tabf, tabi, pick, rowf, rowb, send1, recv1, send2, recv2, wide, acc, en,
    load_sem, orb_sem, out1_sem, in1_sem, out2_sem, in2_sem, en_sem,
):
    me = lax.axis_index("fft")
    band = lax.axis_index("band")
    is_owner = me < NOWN
    before = lax.rem(band + NBAND - 1, NBAND)
    after = lax.rem(band + 1, NBAND)

    loads = [
        pltpu.make_async_copy(src, dst, load_sem.at[i])
        for i, (src, dst) in enumerate(
            ((orb_hbm, own), (taby_hbm, taby), (tabf_hbm, tabf), (tabi_hbm, tabi))
        )
    ]
    for load in loads:
        load.start()

    barrier = pltpu.get_barrier_semaphore()
    pl.semaphore_signal(barrier, inc=1, device_id={"band": before}, device_id_type=MESH)

    @pl.when(is_owner)
    def _():
        def greet(i, carry):
            pl.semaphore_signal(
                barrier, inc=1, device_id={"fft": lax.rem(me + i, NF)}, device_id_type=MESH
            )
            return carry

        lax.fori_loop(1, NF, greet, 0)

    low_iota = lax.broadcasted_iota(jnp.int32, (2 * N, N), 0)
    high_iota = lax.broadcasted_iota(jnp.int32, (N // 2, N), 0)

    def build(o, carry):
        for blk, source in enumerate((owner_device(o), partner_block(o))):
            flat = cols[pl.ds(source, 1), :]
            lanes = pl.ds(pl.multiple_of((2 * o + blk) * N, N), N)
            pick[:, lanes] = jnp.where(low_iota == lax.rem(flat, 2 * N), 1.0, 0.0).astype(bf16)
            high = jnp.where(high_iota == lax.div(flat, 2 * N), f32(1.0), f32(0.0))
            rowf[:, lanes] = high
            rowb[:, lanes] = high.astype(bf16)
        return carry

    lax.fori_loop(0, NOWN, build, 0)

    @pl.when(is_owner)
    def _():
        pl.semaphore_wait(barrier, NOWN)

    @pl.when(jnp.logical_not(is_owner))
    def _():
        pl.semaphore_wait(barrier, NOWN + 1)

    give = pltpu.make_async_remote_copy(
        src_ref=orb_hbm, dst_ref=prev, send_sem=orb_sem.at[0], recv_sem=orb_sem.at[1],
        device_id={"band": after}, device_id_type=MESH,
    )
    give.start()
    for load in loads:
        load.wait()

    def forward(pair, partner, then):
        density = (own[...] * partner[...]).reshape(2 * N, N)
        along = right_table(density, taby[...])
        planes = left_table(tabf[...], jnp.concatenate([along[:N], along[N:]], axis=1))
        half = N // 2
        rows = jnp.concatenate(
            [
                jnp.concatenate([planes[:half, :N], planes[half:, :N]], axis=1),
                jnp.concatenate([planes[:half, N:], planes[half:, N:]], axis=1),
            ],
            axis=0,
        )
        hi, lo = two_terms(rows)
        left = jnp.concatenate([hi, lo], axis=0)

        def step(g, carry):
            lanes = pl.ds(pl.multiple_of(g * LANES, LANES), LANES)
            picked = dot(left, pick[:, lanes])
            mask = rowf[:, lanes]
            for plane in range(2):
                a = plane * half
                both = (picked[a : a + half] + picked[N + a : N + a + half]) * mask
                total = jnp.sum(both, axis=0, keepdims=True)
                for i in range(PER):
                    for blk in range(2):
                        at = (2 * i + blk) * N
                        row = 4 * blk + 2 * pair + plane
                        send1[PER * g + i, row : row + 1, :] = total[:, at : at + N]
            if then is not None:
                for i in range(PER):
                    then(PER * g + i)
            return carry

        lax.fori_loop(0, STEPS, step, 0)

    forward(0, own, None)

    give.wait_recv()

    def out_copy(o):
        return pltpu.make_async_remote_copy(
            src_ref=send1.at[o], dst_ref=recv1.at[me], send_sem=out1_sem, recv_sem=in1_sem,
            device_id={"fft": owner_device(o)}, device_id_type=MESH,
        )

    def send_out(o):
        @pl.when(owner_device(o) != me)
        def _():
            out_copy(o).start()

    forward(1, prev, send_out)

    @pl.when(is_owner)
    def _():
        recv1[me] = send1[me]
        z_iota = signed(lax.broadcasted_iota(jnp.int32, (N, N), 0))
        weights = []
        for source in (me, partner_block(me)):
            flat = cols[pl.ds(source, 1), :]
            row = signed(lax.div(flat, N))
            col = signed(lax.rem(flat, N))
            weights.append(coulomb(z_iota * z_iota + (row * row + col * col)))
        pltpu.make_async_copy(recv1.at[pl.ds(0, NF - 1)], recv1.at[pl.ds(0, NF - 1)], in1_sem).wait()
        got = recv1.reshape(NF * 8, N)
        parts = []
        for q in range(0, 8, 2):
            parts.append(
                jnp.concatenate(
                    [got[pl.ds(q, NF, stride=8), :], got[pl.ds(q + 1, NF, stride=8), :]], axis=0
                )
            )
        spectral = left_table(tabi[...], jnp.concatenate(parts, axis=1))
        v = jnp.concatenate([weights[0], weights[0], weights[1], weights[1]], axis=1)
        weighted = v * spectral
        back = left_table(tabf[...], weighted)
        put = send2.reshape(NF * 8, N)
        for q in range(8):
            a = (q % 2) * NF
            put[pl.ds(q, NF, stride=8), :] = back[a : a + NF, (q // 2) * N : (q // 2 + 1) * N]

        def send_back(i, carry):
            peer = lax.rem(me + i, NF)
            pltpu.make_async_remote_copy(
                src_ref=send2.at[peer], dst_ref=recv2.at[me], send_sem=out2_sem,
                recv_sem=in2_sem.at[me // PER], device_id={"fft": peer}, device_id_type=MESH,
            ).start()
            return carry

        lax.fori_loop(1, NF, send_back, 0)
        recv2[me] = send2[me]
        energy = weighted * spectral
        en[...] = 0.5 * (energy[:, 2 * N : 3 * N] + energy[:, 3 * N :])
        en_copy = pltpu.make_async_remote_copy(
            src_ref=en, dst_ref=spec, send_sem=en_sem.at[0], recv_sem=en_sem.at[1],
            device_id={"fft": partner_block(me)}, device_id_type=MESH,
        )
        en_copy.start()
        spec[...] = 0.5 * (energy[:, :N] + energy[:, N : 2 * N])

    acc[...] = jnp.zeros_like(acc)

    def gather(g, carry):
        holds_me = is_owner & (me // PER == g)
        in_bytes = lambda n: pltpu.make_async_copy(
            recv2.at[pl.ds(0, n)], recv2.at[pl.ds(0, n)], in2_sem.at[g]
        )

        @pl.when(holds_me)
        def _():
            in_bytes(PER - 1).wait()

        @pl.when(jnp.logical_not(holds_me))
        def _():
            in_bytes(PER).wait()

        half = N // 2
        for i in range(PER):
            block = recv2[PER * g + i]
            hi = block.astype(bf16).astype(f32)
            lo = block - hi
            for blk in range(2):
                lanes = pl.ds(pl.multiple_of(g * LANES + (2 * i + blk) * N, N), N)
                mask = rowb[:, lanes].reshape(4, 16, N)
                at = (2 * i + blk) * N
                for term, part in enumerate((hi, lo)):
                    for r in range(4):
                        row = 4 * blk + r
                        one = jnp.broadcast_to(part[row : row + 1], (16, N)).astype(bf16)
                        a = term * 2 * N + r * half
                        wide[a : a + half, at : at + N] = (mask * one[None]).reshape(half, N)
        lanes = pl.ds(pl.multiple_of(g * LANES, LANES), LANES)
        both = lax.dot_general(
            wide[...], pick[:, lanes], (((1,), (1,)), ((), ())), preferred_element_type=f32
        )
        acc[...] += both[: 2 * N] + both[2 * N :]
        return carry

    lax.fori_loop(0, STEPS, gather, 0)

    half = N // 2
    total = None
    for pair, partner in enumerate((own, prev)):
        quarter = [
            [acc[(2 * pair + plane) * half : (2 * pair + plane + 1) * half, p * N : (p + 1) * N] for plane in range(2)]
            for p in range(2)
        ]
        freq = jnp.concatenate([jnp.concatenate(q, axis=1) for q in quarter], axis=0)
        rows = left_table(tabi[...], freq)
        pot = right_table(jnp.concatenate([rows[:, :N], rows[:, N:]], axis=0), taby[...])
        term = pot * partner[...].reshape(2 * N, N)
        total = term if total is None else total + term
    field[...] = (-total).reshape(2, N, N)

    give.wait_send()

    def sent(n, buf, sem):
        pltpu.make_async_copy(buf.at[pl.ds(0, n)], buf.at[pl.ds(0, n)], sem).wait()

    @pl.when(is_owner)
    def _():
        sent(NOWN - 1, send1, out1_sem)
        sent(NF - 1, send2, out2_sem)
        pltpu.make_async_copy(en, en, en_sem.at[0]).wait()

    @pl.when(jnp.logical_not(is_owner))
    def _():
        sent(NOWN, send1, out1_sem)
        pltpu.make_async_copy(en, en, en_sem.at[1]).wait()


def body(orbitals, stick_cols):
    along_y, split_rows, split_cols = tables()
    anywhere = pl.BlockSpec(memory_space=pl.ANY)
    vmem = pl.BlockSpec(memory_space=pltpu.VMEM)
    field, spec = pl.pallas_call(
        kernel,
        out_shape=(
            jax.ShapeDtypeStruct((2, N, N), f32),
            jax.ShapeDtypeStruct((N, N), f32),
        ),
        in_specs=[anywhere, vmem, anywhere, anywhere, anywhere],
        out_specs=(vmem, vmem),
        scratch_shapes=[
            pltpu.VMEM((2, N, N), f32),
            pltpu.VMEM((2, N, N), f32),
            pltpu.VMEM((2 * N, 2 * N), bf16),
            pltpu.VMEM((2 * N, 2 * N), bf16),
            pltpu.VMEM((2 * N, 2 * N), bf16),
            pltpu.VMEM((2 * N, NF * N), bf16),
            pltpu.VMEM((N // 2, NF * N), f32),
            pltpu.VMEM((N // 2, NF * N), bf16),
            pltpu.VMEM((NOWN, 8, N), f32),
            pltpu.VMEM((NF, 8, N), f32),
            pltpu.VMEM((NF, 8, N), f32),
            pltpu.VMEM((NOWN, 8, N), f32),
            pltpu.VMEM((4 * N, LANES), bf16),
            pltpu.VMEM((2 * N, 2 * N), f32),
            pltpu.VMEM((N, N), f32),
            pltpu.SemaphoreType.DMA((4,)),
            pltpu.SemaphoreType.DMA((2,)),
            pltpu.SemaphoreType.DMA,
            pltpu.SemaphoreType.DMA,
            pltpu.SemaphoreType.DMA,
            pltpu.SemaphoreType.DMA((STEPS,)),
            pltpu.SemaphoreType.DMA((2,)),
        ],
        compiler_params=pltpu.CompilerParams(
            collective_id=0, has_side_effects=True, vmem_limit_bytes=40 << 20
        ),
        name="exchange",
    )(
        orbitals.reshape(2, N, N),
        stick_cols.reshape(NF, N),
        jnp.asarray(along_y),
        jnp.asarray(split_rows),
        jnp.asarray(split_cols),
    )
    return field[None], spec[None]


def solution(mesh):
    return jax.shard_map(
        body,
        mesh=mesh,
        in_specs=(P("band", "fft", None, None), P()),
        out_specs=(P("band", "fft", None, None), P("band", None, "fft")),
        check_vma=False,
    )
```

```python
import functools
import math

import jax
import jax.numpy as jnp
import ml_dtypes
import numpy as np
from jax import lax
from jax.experimental import pallas as pl
from jax.experimental.pallas import tpu as pltpu
from jax.sharding import PartitionSpec as P

RAD = 48
N = 128
NF = 64
NBAND = 4
NOWN = 32
PER = 4
STEPS = NOWN // PER
LANES = PER * 2 * N
TILES = 5
ROWS = 8 * TILES

screening = 16.0
strength = 10.0

MESH = pl.DeviceIdType.MESH
f32 = jnp.float32
bf16 = jnp.bfloat16


def owner_device(o):
    return o // 2 * 4 + o % 2


def owner_index(f):
    return f // 4 * 2 + f % 4


def owns(f):
    return f % 4 < 2


def partner_block(o):
    return o // 2 * 4 + 3 - o % 2


def back_step(me, i):
    t = (i + 1) // 2
    return (me // 8 + t * (1 - 2 * (i % 2)) + 8) % 8


def tables():
    k = np.arange(N)
    angles = 2.0 * math.pi / N * (k[:, None] * k[None, :] % N)
    c = (np.cos(angles) + np.sin(angles)) / math.sqrt(N)

    def terms(x):
        hi = x.astype(np.float32).astype(ml_dtypes.bfloat16)
        lo = (x - hi.astype(np.float64)).astype(np.float32).astype(ml_dtypes.bfloat16)
        return hi, lo

    def left(x):
        hi, lo = terms(x)
        return np.block([[hi, hi], [lo, lo]])

    def right(x):
        hi, lo = terms(x)
        return np.block([[hi, lo], [hi, lo]])

    by_b = np.zeros((N, N))
    by_b[:, : 2 * RAD + 1] = c[:, (np.arange(2 * RAD + 1) - RAD) % N]
    by_a = np.zeros((N, N))
    for sub in range(8):
        for t in range(16):
            index = 8 * t + sub if t < 12 else 8 * (t - 4) + sub
            if sub == 7 and t >= 12:
                index = 2 * RAD if t == 15 else None
            if index is not None:
                by_a[16 * sub + t] = c[(index - RAD) % N]
    order = np.concatenate([k[0::2], k[1::2]])
    return np.stack(
        [right(by_b), left(by_a), left(c[:, order]), left(c[order]), left(by_a.T), right(by_b.T)]
    )


def two_terms(x):
    hi = x.astype(bf16)
    return hi, (x - hi.astype(f32)).astype(bf16)


def signed(x):
    return jnp.where(x < N // 2, x, x - N)


def coulomb(squared):
    kappa = squared.astype(f32)
    safe = jnp.maximum(kappa, f32(1.0))
    values = strength * screening * (1.0 - jnp.exp(-kappa / screening)) / safe
    inside = (squared > 0) & (squared <= RAD * RAD)
    return jnp.where(inside, values, f32(0.0))


def dot(a, b):
    return jnp.dot(a, b, preferred_element_type=f32)


def left_table(table, x):
    hi, lo = two_terms(x)
    both = dot(table, jnp.concatenate([hi, lo], axis=0))
    return both[:N] + both[N:]


def right_table(x, table):
    hi, lo = two_terms(x)
    both = dot(jnp.concatenate([hi, lo], axis=1), table)
    return both[:, :N] + both[:, N:]


def turn(x, groups):
    return x if groups % 4 == 0 else pltpu.roll(x, groups % 4 * 32, axis=1)


def masks():
    group = lax.broadcasted_iota(jnp.int32, (8, N), 1) // 32
    row = lax.broadcasted_iota(jnp.int32, (8, N), 0)
    return [group == i for i in range(4)], row < 4, row == 7


def by_group(groups, parts):
    low = jnp.where(groups[0], parts[0], parts[1])
    high = jnp.where(groups[2], parts[2], parts[3])
    return jnp.where(groups[0] | groups[1], low, high)


def pack(plane):
    groups, upper, last = masks()
    tiles = [[], [], [], [], []]
    for h in range(2):
        parts = [[], [], [], [], []]
        for i in range(4):
            sub = 4 * h + i
            main = plane[16 * sub : 16 * sub + 8]
            rest = plane[16 * sub + 8 : 16 * sub + 16]
            for y in range(3):
                parts[y].append(turn(main, i - y))
            second = turn(rest, i - 1)
            moved = pltpu.roll(second, 4, axis=0) if sub == 7 else second
            parts[3].append(jnp.where(upper, turn(rest, i), moved))
            third = turn(rest, i - 2)
            if sub == 0:
                third = jnp.where(upper, third, turn(main, i - 3))
            if sub == 7:
                third = jnp.where(last, second, third)
            parts[4].append(third)
        for t in range(TILES):
            tiles[t].append(by_group(groups, parts[t]))
    return [jnp.concatenate(t, axis=1) for t in tiles]


def unpack(tiles):
    groups, upper, last = masks()
    zero = jnp.zeros((8, N), f32)
    out = []
    for sub in range(8):
        h, i = sub // 4, sub % 4
        t0, t1, t2, t3, t4 = (t[:, h * N : (h + 1) * N] for t in tiles)
        special = zero
        if sub == 0:
            special = jnp.where(upper, zero, turn(t4, 3 - i))
        out.append(by_group(groups, [turn(t0, -i), turn(t1, 1 - i), turn(t2, 2 - i), special]))
        first = jnp.where(upper, turn(t3, -i), zero)
        third = jnp.where(upper, turn(t4, 2 - i), zero)
        second = turn(t3, 1 - i)
        if sub == 7:
            second = jnp.where(
                upper, pltpu.roll(second, 4, axis=0), jnp.where(last, turn(t4, 1 - i), zero)
            )
        else:
            second = jnp.where(upper, zero, second)
        out.append(by_group(groups, [first, second, third, zero]))
    return jnp.concatenate(out, axis=0)


def kernel(
    orb_hbm, cols_hbm, tab_hbm, field, spec,
    cols, places, lanes_of, own, prev, tab, pick, rowf, rowb, send1, recv1, send2, recv2, wide, acc, en,
    load_sem, orb_sem, out1_sem, in1_sem, out2_sem, in2_sem, en_sem,
):
    me = lax.axis_index("fft")
    band = lax.axis_index("band")
    is_owner = owns(me)
    mine = owner_index(me)
    before = lax.rem(band + NBAND - 1, NBAND)
    after = lax.rem(band + 1, NBAND)

    loads = [
        pltpu.make_async_copy(src, dst, load_sem.at[i])
        for i, (src, dst) in enumerate(((cols_hbm, cols), (orb_hbm, own), (tab_hbm, tab)))
    ]
    y_to, x_to, z_to, z_from, x_from, y_from = (tab.at[i] for i in range(6))
    for load in loads:
        load.start()

    barrier = pltpu.get_barrier_semaphore()
    pl.semaphore_signal(barrier, inc=1, device_id={"band": before}, device_id_type=MESH)

    @pl.when(is_owner)
    def _():
        def greet(i, carry):
            pl.semaphore_signal(
                barrier, inc=1, device_id={"fft": lax.rem(me + i, NF)}, device_id_type=MESH
            )
            return carry

        lax.fori_loop(1, NF, greet, 0)

    loads[0].wait()
    flat = cols[...]
    along_a = signed(lax.div(flat, N)) + RAD
    along_b = signed(lax.rem(flat, N)) + RAD
    inside = (along_a >= 0) & (along_a < 2 * RAD) & (along_b >= 0) & (along_b < 2 * RAD)
    big_a, big_b = along_a >> 3, along_b >> 5
    row = jnp.where(big_a < 8, 8 * big_b + big_a, 16 + 4 * big_b + big_a)
    row = jnp.where(inside, row, -1)
    lane = 32 * (along_a & 7) + (along_b & 31)
    top = (along_a == RAD) & (along_b == 2 * RAD)
    side = (along_a == 2 * RAD) & (along_b == RAD)
    places[...] = jnp.where(top, 38, jnp.where(side, 39, row))
    lanes_of[...] = jnp.where(top, 0, jnp.where(side, 240, lane))
    low_iota = lax.broadcasted_iota(jnp.int32, (2 * N, N), 0)
    row_iota = lax.broadcasted_iota(jnp.int32, (ROWS, N), 0)
    twice = lax.broadcasted_iota(jnp.int32, (2 * ROWS, N), 0)
    twice = 8 * lax.div(twice, 16) + lax.rem(twice, 8)

    def build(o):
        for blk, source in enumerate((owner_device(o), partner_block(o))):
            place = places[pl.ds(source, 1), :]
            lanes = pl.ds(pl.multiple_of((2 * o + blk) * N, N), N)
            pick[:, lanes] = jnp.where(low_iota == lanes_of[pl.ds(source, 1), :], 1.0, 0.0).astype(bf16)
            rowf[:, lanes] = jnp.where(row_iota == place, f32(1.0), f32(0.0))
            rowb[:, lanes] = jnp.where(twice == place, 1.0, 0.0).astype(bf16)

    lax.fori_loop(0, NOWN, lambda o, c: (build(o), c)[1], 0)

    @pl.when(is_owner)
    def _():
        pl.semaphore_wait(barrier, NOWN)

    @pl.when(jnp.logical_not(is_owner))
    def _():
        pl.semaphore_wait(barrier, NOWN + 1)

    give = pltpu.make_async_remote_copy(
        src_ref=orb_hbm, dst_ref=prev, send_sem=orb_sem.at[0], recv_sem=orb_sem.at[1],
        device_id={"band": after}, device_id_type=MESH,
    )
    give.start()

    for load in loads[1:]:
        load.wait()

    def forward(pair, partner, then):
        density = (own[...] * partner[...]).reshape(2 * N, N)
        along = right_table(density, y_to[...])
        planes = left_table(x_to[...], jnp.concatenate([along[:N], along[N:]], axis=1))
        packed = [pack(planes[:, :N]), pack(planes[:, N:])]
        rows = jnp.concatenate([packed[p][t] for t in range(TILES) for p in range(2)], axis=0)
        hi, lo = two_terms(rows)
        left = jnp.concatenate([hi, lo], axis=0)

        def step(i, carry):
            g = STEPS - 1 - i
            lanes = pl.ds(pl.multiple_of(g * LANES, LANES), LANES)
            picked = dot(left, pick[:, lanes])
            for plane in range(2):
                sums = None
                for t in range(TILES):
                    a = 16 * t + 8 * plane
                    both = picked[a : a + 8] + picked[2 * ROWS + a : 2 * ROWS + a + 8]
                    both = both * rowf[8 * t : 8 * t + 8, lanes]
                    sums = both if sums is None else sums + both
                total = jnp.sum(sums, axis=0, keepdims=True)
                for i in range(PER):
                    for blk in range(2):
                        at = (2 * i + blk) * N
                        row = 4 * blk + 2 * pair + plane
                        send1[PER * g + i, row : row + 1, :] = total[:, at : at + N]
            if then is not None:
                for i in range(PER):
                    then(PER * g + i)
            return carry

        lax.fori_loop(0, STEPS, step, 0)

    forward(0, own, None)

    give.wait_recv()

    def out_copy(o):
        return pltpu.make_async_remote_copy(
            src_ref=send1.at[o], dst_ref=recv1.at[me], send_sem=out1_sem, recv_sem=in1_sem,
            device_id={"fft": owner_device(o)}, device_id_type=MESH,
        )

    def send_out(o):
        @pl.when(owner_device(o) != me)
        def _():
            out_copy(o).start()

    forward(1, prev, send_out)

    @pl.when(is_owner)
    def _():
        recv1[me] = send1[mine]
        z_iota = signed(lax.broadcasted_iota(jnp.int32, (N, N), 0))
        weights = []
        for source in (me, partner_block(mine)):
            flat = cols[pl.ds(source, 1), :]
            row = signed(lax.div(flat, N))
            col = signed(lax.rem(flat, N))
            weights.append(coulomb(z_iota * z_iota + (row * row + col * col)))
        pltpu.make_async_copy(recv1.at[pl.ds(0, NF - 1)], recv1.at[pl.ds(0, NF - 1)], in1_sem).wait()
        got = recv1.reshape(NF * 8, N)
        parts = []
        for q in range(0, 8, 2):
            parts.append(
                jnp.concatenate(
                    [got[pl.ds(q, NF, stride=8), :], got[pl.ds(q + 1, NF, stride=8), :]], axis=0
                )
            )
        spectral = left_table(z_to[...], jnp.concatenate(parts, axis=1))
        v = jnp.concatenate([weights[0], weights[0], weights[1], weights[1]], axis=1)
        weighted = v * spectral
        back = left_table(z_from[...], weighted)
        put = send2.reshape(NF * 8, N)
        for q in range(8):
            a = (q % 2) * NF
            put[pl.ds(q, NF, stride=8), :] = back[a : a + NF, (q // 2) * N : (q // 2 + 1) * N]

        def send_back(z, carry):
            for k in range(8):
                peer = z * 8 + k

                @pl.when(peer != me)
                def _():
                    pltpu.make_async_remote_copy(
                        src_ref=send2.at[peer], dst_ref=recv2.at[mine], send_sem=out2_sem,
                        recv_sem=in2_sem.at[mine // PER], device_id={"fft": peer},
                        device_id_type=MESH,
                    ).start()

            return carry

        lax.fori_loop(0, NF // 8, send_back, 0)
        recv2[mine] = send2[me]
        energy = weighted * spectral
        en[...] = 0.5 * (energy[:, 2 * N : 3 * N] + energy[:, 3 * N :])
        en_copy = pltpu.make_async_remote_copy(
            src_ref=en, dst_ref=spec, send_sem=en_sem.at[0], recv_sem=en_sem.at[1],
            device_id={"fft": partner_block(mine)}, device_id_type=MESH,
        )
        en_copy.start()
        spec[...] = 0.5 * (energy[:, :N] + energy[:, N : 2 * N])

    acc[...] = jnp.zeros_like(acc)

    def gather(i, carry):
        g = back_step(me, i)
        holds_me = is_owner & (mine // PER == g)
        in_bytes = lambda n: pltpu.make_async_copy(
            recv2.at[pl.ds(0, n)], recv2.at[pl.ds(0, n)], in2_sem.at[g]
        )

        @pl.when(holds_me)
        def _():
            in_bytes(PER - 1).wait()

        @pl.when(jnp.logical_not(holds_me))
        def _():
            in_bytes(PER).wait()

        for i in range(PER):
            block = recv2[PER * g + i]
            hi = block.astype(bf16).astype(f32)
            lo = block - hi
            for blk in range(2):
                lanes = pl.ds(pl.multiple_of(g * LANES + (2 * i + blk) * N, N), N)
                at = (2 * i + blk) * N
                for term, part in enumerate((hi, lo)):
                    for r in range(0, 4, 2):
                        row = 4 * blk + r
                        two = [jnp.broadcast_to(part[q : q + 1], (8, N)) for q in (row, row + 1)]
                        one = jnp.concatenate(two, axis=0).astype(bf16)
                        for t in range(TILES):
                            a = term * 4 * ROWS + 32 * t + 8 * r
                            wide[a : a + 16, at : at + N] = rowb[16 * t : 16 * t + 16, lanes] * one
        lanes = pl.ds(pl.multiple_of(g * LANES, LANES), LANES)
        both = lax.dot_general(
            wide[...], pick[:, lanes], (((1,), (1,)), ((), ())), preferred_element_type=f32
        )
        acc[...] += both[: 4 * ROWS] + both[4 * ROWS :]
        return carry

    lax.fori_loop(0, STEPS, gather, 0)

    total = None
    for pair, partner in enumerate((own, prev)):
        freq = jnp.concatenate(
            [
                unpack([acc[32 * t + 8 * r : 32 * t + 8 * r + 8, :] for t in range(TILES)])
                for r in (2 * pair, 2 * pair + 1)
            ],
            axis=1,
        )
        rows = left_table(x_from[...], freq)
        pot = right_table(jnp.concatenate([rows[:, :N], rows[:, N:]], axis=0), y_from[...])
        term = pot * partner[...].reshape(2 * N, N)
        total = term if total is None else total + term
    field[...] = (-total).reshape(2, N, N)

    give.wait_send()

    def sent(n, buf, sem):
        pltpu.make_async_copy(buf.at[pl.ds(0, n)], buf.at[pl.ds(0, n)], sem).wait()

    @pl.when(is_owner)
    def _():
        sent(NOWN - 1, send1, out1_sem)
        sent(NF - 1, send2, out2_sem)
        pltpu.make_async_copy(en, en, en_sem.at[0]).wait()

    @pl.when(jnp.logical_not(is_owner))
    def _():
        sent(NOWN, send1, out1_sem)
        pltpu.make_async_copy(en, en, en_sem.at[1]).wait()


def body(orbitals, stick_cols):
    anywhere = pl.BlockSpec(memory_space=pltpu.HBM)
    vmem = pl.BlockSpec(memory_space=pltpu.VMEM)
    field, spec = pl.pallas_call(
        kernel,
        out_shape=(
            jax.ShapeDtypeStruct((2, N, N), f32),
            jax.ShapeDtypeStruct((N, N), f32),
        ),
        in_specs=[anywhere] * 3,
        out_specs=(vmem, vmem),
        scratch_shapes=[
            pltpu.VMEM((NF, N), jnp.int32),
            pltpu.VMEM((NF, N), jnp.int32),
            pltpu.VMEM((NF, N), jnp.int32),
            pltpu.VMEM((2, N, N), f32),
            pltpu.VMEM((2, N, N), f32),
            pltpu.VMEM((6, 2 * N, 2 * N), bf16),
            pltpu.VMEM((2 * N, NF * N), bf16),
            pltpu.VMEM((ROWS, NF * N), f32),
            pltpu.VMEM((2 * ROWS, NF * N), bf16),
            pltpu.VMEM((NOWN, 8, N), f32),
            pltpu.VMEM((NF, 8, N), f32),
            pltpu.VMEM((NF, 8, N), f32),
            pltpu.VMEM((NOWN, 8, N), f32),
            pltpu.VMEM((8 * ROWS, LANES), bf16),
            pltpu.VMEM((4 * ROWS, 2 * N), f32),
            pltpu.VMEM((N, N), f32),
            pltpu.SemaphoreType.DMA((3,)),
            pltpu.SemaphoreType.DMA((2,)),
            pltpu.SemaphoreType.DMA,
            pltpu.SemaphoreType.DMA,
            pltpu.SemaphoreType.DMA,
            pltpu.SemaphoreType.DMA((STEPS,)),
            pltpu.SemaphoreType.DMA((2,)),
        ],
        compiler_params=pltpu.CompilerParams(
            collective_id=0, has_side_effects=True, vmem_limit_bytes=(64 << 20) - (10615 << 10)
        ),
        name="exchange",
    )(
        orbitals.reshape(2, N, N),
        stick_cols.reshape(NF, N),
        jnp.asarray(tables()),
    )
    return field[None], spec[None]


def solution(mesh):
    return jax.shard_map(
        body,
        mesh=mesh,
        in_specs=(P("band", "fft", None, None), P()),
        out_specs=(P("band", "fft", None, None), P("band", None, "fft")),
        check_vma=False,
    )
```

```python
import functools
import math

import jax
import jax.numpy as jnp
import ml_dtypes
import numpy as np
from jax import lax
from jax.experimental import pallas as pl
from jax.experimental.pallas import tpu as pltpu
from jax.sharding import PartitionSpec as P

RAD = 48
N = 128
NF = 64
NBAND = 4
NOWN = 32
PER = 8
STEPS = NOWN // PER
LANES = PER * 2 * N
TILES = 5
ROWS = 8 * TILES

screening = 16.0
strength = 10.0

MESH = pl.DeviceIdType.MESH
f32 = jnp.float32
bf16 = jnp.bfloat16


def owner_device(o):
    return o // 2 * 4 + o % 2


def owner_index(f):
    return f // 4 * 2 + f % 4


def owns(f):
    return f % 4 < 2


def partner_block(o):
    return o // 2 * 4 + 3 - o % 2


def back_step(me, i):
    t = (i + 1) // 2
    return (me // 16 + t * (1 - 2 * (i % 2)) + 4) % 4


def tables():
    k = np.arange(N)
    angles = 2.0 * math.pi / N * (k[:, None] * k[None, :] % N)
    c = (np.cos(angles) + np.sin(angles)) / math.sqrt(N)

    def terms(x):
        hi = x.astype(np.float32).astype(ml_dtypes.bfloat16)
        lo = (x - hi.astype(np.float64)).astype(np.float32).astype(ml_dtypes.bfloat16)
        return hi, lo

    def left(x):
        hi, lo = terms(x)
        return np.block([[hi, hi], [lo, lo]])

    def right(x):
        hi, lo = terms(x)
        return np.block([[hi, lo], [hi, lo]])

    by_b = np.zeros((N, N))
    by_b[:, : 2 * RAD + 1] = c[:, (np.arange(2 * RAD + 1) - RAD) % N]
    by_a = np.zeros((N, N))
    for sub in range(8):
        for t in range(16):
            index = 8 * t + sub if t < 12 else 8 * (t - 4) + sub
            if sub == 7 and t >= 12:
                index = 2 * RAD if t == 15 else None
            if index is not None:
                by_a[16 * sub + t] = c[(index - RAD) % N]
    order = np.concatenate([k[0::2], k[1::2]])
    return np.stack(
        [right(by_b), left(by_a), left(c[:, order]), left(c[order]), left(by_a.T), right(by_b.T)]
    )


def two_terms(x):
    hi = x.astype(bf16)
    return hi, (x - hi.astype(f32)).astype(bf16)


def signed(x):
    return jnp.where(x < N // 2, x, x - N)


def coulomb(squared):
    kappa = squared.astype(f32)
    safe = jnp.maximum(kappa, f32(1.0))
    values = strength * screening * (1.0 - jnp.exp(-kappa / screening)) / safe
    inside = (squared > 0) & (squared <= RAD * RAD)
    return jnp.where(inside, values, f32(0.0))


def dot(a, b):
    return jnp.dot(a, b, preferred_element_type=f32)


def left_table(table, x):
    hi, lo = two_terms(x)
    both = dot(table, jnp.concatenate([hi, lo], axis=0))
    return both[:N] + both[N:]


def right_table(x, table):
    hi, lo = two_terms(x)
    both = dot(jnp.concatenate([hi, lo], axis=1), table)
    return both[:, :N] + both[:, N:]


def turn(x, groups):
    return x if groups % 4 == 0 else pltpu.roll(x, groups % 4 * 32, axis=1)


def masks():
    group = lax.broadcasted_iota(jnp.int32, (8, N), 1) // 32
    row = lax.broadcasted_iota(jnp.int32, (8, N), 0)
    return [group == i for i in range(4)], row < 4, row == 7


def by_group(groups, parts):
    low = jnp.where(groups[0], parts[0], parts[1])
    high = jnp.where(groups[2], parts[2], parts[3])
    return jnp.where(groups[0] | groups[1], low, high)


def pack(plane):
    groups, upper, last = masks()
    tiles = [[], [], [], [], []]
    for h in range(2):
        parts = [[], [], [], [], []]
        for i in range(4):
            sub = 4 * h + i
            main = plane[16 * sub : 16 * sub + 8]
            rest = plane[16 * sub + 8 : 16 * sub + 16]
            for y in range(3):
                parts[y].append(turn(main, i - y))
            second = turn(rest, i - 1)
            moved = pltpu.roll(second, 4, axis=0) if sub == 7 else second
            parts[3].append(jnp.where(upper, turn(rest, i), moved))
            third = turn(rest, i - 2)
            if sub == 0:
                third = jnp.where(upper, third, turn(main, i - 3))
            if sub == 7:
                third = jnp.where(last, second, third)
            parts[4].append(third)
        for t in range(TILES):
            tiles[t].append(by_group(groups, parts[t]))
    return [jnp.concatenate(t, axis=1) for t in tiles]


def unpack(tiles):
    groups, upper, last = masks()
    zero = jnp.zeros((8, N), f32)
    out = []
    for sub in range(8):
        h, i = sub // 4, sub % 4
        t0, t1, t2, t3, t4 = (t[:, h * N : (h + 1) * N] for t in tiles)
        special = zero
        if sub == 0:
            special = jnp.where(upper, zero, turn(t4, 3 - i))
        out.append(by_group(groups, [turn(t0, -i), turn(t1, 1 - i), turn(t2, 2 - i), special]))
        first = jnp.where(upper, turn(t3, -i), zero)
        third = jnp.where(upper, turn(t4, 2 - i), zero)
        second = turn(t3, 1 - i)
        if sub == 7:
            second = jnp.where(
                upper, pltpu.roll(second, 4, axis=0), jnp.where(last, turn(t4, 1 - i), zero)
            )
        else:
            second = jnp.where(upper, zero, second)
        out.append(by_group(groups, [first, second, third, zero]))
    return jnp.concatenate(out, axis=0)


def kernel(
    orb_hbm, cols_hbm, tab_hbm, field, spec,
    cols, places, lanes_of, own, prev, tab, pick, rowf, rowb, send1, recv1, send2, recv2, wide, acc, en,
    load_sem, orb_sem, out1_sem, in1_sem, out2_sem, in2_sem, en_sem,
):
    me = lax.axis_index("fft")
    band = lax.axis_index("band")
    is_owner = owns(me)
    mine = owner_index(me)
    before = lax.rem(band + NBAND - 1, NBAND)
    after = lax.rem(band + 1, NBAND)

    barrier = pltpu.get_barrier_semaphore()
    pl.semaphore_signal(barrier, inc=1, device_id={"band": before}, device_id_type=MESH)

    @pl.when(is_owner)
    def _():
        def greet(z, carry):
            for k in range(8):

                @pl.when(z * 8 + k != me)
                def _():
                    pl.semaphore_signal(
                        barrier, inc=1, device_id={"fft": z * 8 + k}, device_id_type=MESH
                    )

            return carry

        lax.fori_loop(0, NF // 8, greet, 0)

    loads = [
        pltpu.make_async_copy(src, dst, load_sem.at[i])
        for i, (src, dst) in enumerate(((cols_hbm, cols), (orb_hbm, own), (tab_hbm, tab)))
    ]
    y_to, x_to, z_to, z_from, x_from, y_from = (tab.at[i] for i in range(6))
    for load in loads:
        load.start()

    loads[0].wait()
    flat = cols[...]
    along_a = signed(lax.div(flat, N)) + RAD
    along_b = signed(lax.rem(flat, N)) + RAD
    inside = (along_a >= 0) & (along_a < 2 * RAD) & (along_b >= 0) & (along_b < 2 * RAD)
    big_a, big_b = along_a >> 3, along_b >> 5
    row = jnp.where(big_a < 8, 8 * big_b + big_a, 16 + 4 * big_b + big_a)
    row = jnp.where(inside, row, -1)
    lane = 32 * (along_a & 7) + (along_b & 31)
    top = (along_a == RAD) & (along_b == 2 * RAD)
    side = (along_a == 2 * RAD) & (along_b == RAD)
    places[...] = jnp.where(top, 38, jnp.where(side, 39, row))
    lanes_of[...] = jnp.where(top, 0, jnp.where(side, 240, lane))
    low_iota = lax.broadcasted_iota(jnp.int32, (2 * N, N), 0)
    row_iota = lax.broadcasted_iota(jnp.int32, (ROWS, N), 0)
    twice = lax.broadcasted_iota(jnp.int32, (2 * ROWS, N), 0)
    twice = 8 * lax.div(twice, 16) + lax.rem(twice, 8)

    def build(o):
        for blk, source in enumerate((owner_device(o), partner_block(o))):
            place = places[pl.ds(source, 1), :]
            lanes = pl.ds(pl.multiple_of((2 * o + blk) * N, N), N)
            pick[:, lanes] = jnp.where(low_iota == lanes_of[pl.ds(source, 1), :], 1.0, 0.0).astype(bf16)
            rowf[:, lanes] = jnp.where(row_iota == place, f32(1.0), f32(0.0))
            rowb[:, lanes] = jnp.where(twice == place, 1.0, 0.0).astype(bf16)

    lax.fori_loop(0, NOWN, lambda o, c: (build(o), c)[1], 0)

    @pl.when(is_owner)
    def _():
        pl.semaphore_wait(barrier, NOWN)

    @pl.when(jnp.logical_not(is_owner))
    def _():
        pl.semaphore_wait(barrier, NOWN + 1)

    give = pltpu.make_async_remote_copy(
        src_ref=own, dst_ref=prev, send_sem=orb_sem.at[0], recv_sem=orb_sem.at[1],
        device_id={"band": after}, device_id_type=MESH,
    )
    loads[1].wait()
    give.start()

    loads[2].wait()

    def forward(pair, partner, then):
        density = (own[...] * partner[...]).reshape(2 * N, N)
        along = right_table(density, y_to[...])
        planes = left_table(x_to[...], jnp.concatenate([along[:N], along[N:]], axis=1))
        packed = [pack(planes[:, :N]), pack(planes[:, N:])]
        rows = jnp.concatenate([packed[p][t] for t in range(TILES) for p in range(2)], axis=0)
        hi, lo = two_terms(rows)
        left = jnp.concatenate([hi, lo], axis=0)

        def step(i, carry):
            g = STEPS - 1 - i
            lanes = pl.ds(pl.multiple_of(g * LANES, LANES), LANES)
            picked = dot(left, pick[:, lanes])
            for plane in range(2):
                sums = None
                for t in range(TILES):
                    a = 16 * t + 8 * plane
                    both = picked[a : a + 8] + picked[2 * ROWS + a : 2 * ROWS + a + 8]
                    both = both * rowf[8 * t : 8 * t + 8, lanes]
                    sums = both if sums is None else sums + both
                total = jnp.sum(sums, axis=0, keepdims=True)
                for i in range(PER):
                    for blk in range(2):
                        at = (2 * i + blk) * N
                        row = 4 * blk + 2 * pair + plane
                        send1[PER * g + i, row : row + 1, :] = total[:, at : at + N]
            if then is not None:
                for i in range(PER):
                    then(PER * g + i)
            return carry

        lax.fori_loop(0, STEPS, step, 0)

    forward(0, own, None)

    give.wait_recv()

    def out_copy(o):
        return pltpu.make_async_remote_copy(
            src_ref=send1.at[o], dst_ref=recv1.at[me], send_sem=out1_sem, recv_sem=in1_sem,
            device_id={"fft": owner_device(o)}, device_id_type=MESH,
        )

    def send_out(o):
        @pl.when(owner_device(o) != me)
        def _():
            out_copy(o).start()

    forward(1, prev, send_out)

    @pl.when(is_owner)
    def _():
        recv1[me] = send1[mine]
        z_iota = signed(lax.broadcasted_iota(jnp.int32, (N, N), 0))
        weights = []
        for source in (me, partner_block(mine)):
            flat = cols[pl.ds(source, 1), :]
            row = signed(lax.div(flat, N))
            col = signed(lax.rem(flat, N))
            weights.append(coulomb(z_iota * z_iota + (row * row + col * col)))
        pltpu.make_async_copy(recv1.at[pl.ds(0, NF - 1)], recv1.at[pl.ds(0, NF - 1)], in1_sem).wait()
        got = recv1.reshape(NF * 8, N)
        parts = []
        for q in range(0, 8, 2):
            parts.append(
                jnp.concatenate(
                    [got[pl.ds(q, NF, stride=8), :], got[pl.ds(q + 1, NF, stride=8), :]], axis=0
                )
            )
        spectral = left_table(z_to[...], jnp.concatenate(parts, axis=1))
        v = jnp.concatenate([weights[0], weights[0], weights[1], weights[1]], axis=1)
        weighted = v * spectral
        back = left_table(z_from[...], weighted)
        put = send2.reshape(NF * 8, N)
        for q in range(8):
            a = (q % 2) * NF
            put[pl.ds(q, NF, stride=8), :] = back[a : a + NF, (q // 2) * N : (q // 2 + 1) * N]

        def send_back(z, carry):
            for k in range(8):
                peer = z * 8 + k

                @pl.when(peer != me)
                def _():
                    pltpu.make_async_remote_copy(
                        src_ref=send2.at[peer], dst_ref=recv2.at[mine], send_sem=out2_sem,
                        recv_sem=in2_sem.at[mine // PER], device_id={"fft": peer},
                        device_id_type=MESH,
                    ).start()

            return carry

        lax.fori_loop(0, NF // 8, send_back, 0)
        recv2[mine] = send2[me]
        energy = weighted * spectral
        en[...] = 0.5 * (energy[:, 2 * N : 3 * N] + energy[:, 3 * N :])
        en_copy = pltpu.make_async_remote_copy(
            src_ref=en, dst_ref=spec, send_sem=en_sem.at[0], recv_sem=en_sem.at[1],
            device_id={"fft": partner_block(mine)}, device_id_type=MESH,
        )
        en_copy.start()
        spec[...] = 0.5 * (energy[:, :N] + energy[:, N : 2 * N])

    acc[...] = jnp.zeros_like(acc)

    def gather(i, carry):
        g = back_step(me, i)
        holds_me = is_owner & (mine // PER == g)
        in_bytes = lambda n: pltpu.make_async_copy(
            recv2.at[pl.ds(0, n)], recv2.at[pl.ds(0, n)], in2_sem.at[g]
        )

        @pl.when(holds_me)
        def _():
            in_bytes(PER - 1).wait()

        @pl.when(jnp.logical_not(holds_me))
        def _():
            in_bytes(PER).wait()

        for i in range(PER):
            block = recv2[PER * g + i]
            hi = block.astype(bf16).astype(f32)
            lo = block - hi
            for blk in range(2):
                lanes = pl.ds(pl.multiple_of(g * LANES + (2 * i + blk) * N, N), N)
                at = (2 * i + blk) * N
                for term, part in enumerate((hi, lo)):
                    for r in range(0, 4, 2):
                        row = 4 * blk + r
                        two = [jnp.broadcast_to(part[q : q + 1], (8, N)) for q in (row, row + 1)]
                        one = jnp.concatenate(two, axis=0).astype(bf16)
                        for t in range(TILES):
                            a = term * 4 * ROWS + 32 * t + 8 * r
                            wide[a : a + 16, at : at + N] = rowb[16 * t : 16 * t + 16, lanes] * one
        lanes = pl.ds(pl.multiple_of(g * LANES, LANES), LANES)
        both = lax.dot_general(
            wide[...], pick[:, lanes], (((1,), (1,)), ((), ())), preferred_element_type=f32
        )
        acc[...] += both[: 4 * ROWS] + both[4 * ROWS :]
        return carry

    lax.fori_loop(0, STEPS, gather, 0)

    total = None
    for pair, partner in enumerate((own, prev)):
        freq = jnp.concatenate(
            [
                unpack([acc[32 * t + 8 * r : 32 * t + 8 * r + 8, :] for t in range(TILES)])
                for r in (2 * pair, 2 * pair + 1)
            ],
            axis=1,
        )
        rows = left_table(x_from[...], freq)
        pot = right_table(jnp.concatenate([rows[:, :N], rows[:, N:]], axis=0), y_from[...])
        term = pot * partner[...].reshape(2 * N, N)
        total = term if total is None else total + term
    field[...] = (-total).reshape(2, N, N)

    give.wait_send()

    def sent(n, buf, sem):
        pltpu.make_async_copy(buf.at[pl.ds(0, n)], buf.at[pl.ds(0, n)], sem).wait()

    @pl.when(is_owner)
    def _():
        sent(NOWN - 1, send1, out1_sem)
        sent(NF - 1, send2, out2_sem)
        pltpu.make_async_copy(en, en, en_sem.at[0]).wait()

    @pl.when(jnp.logical_not(is_owner))
    def _():
        sent(NOWN, send1, out1_sem)
        pltpu.make_async_copy(en, en, en_sem.at[1]).wait()


def body(orbitals, stick_cols):
    anywhere = pl.BlockSpec(memory_space=pltpu.HBM)
    vmem = pl.BlockSpec(memory_space=pltpu.VMEM)
    field, spec = pl.pallas_call(
        kernel,
        out_shape=(
            jax.ShapeDtypeStruct((2, N, N), f32),
            jax.ShapeDtypeStruct((N, N), f32),
        ),
        in_specs=[anywhere] * 3,
        out_specs=(vmem, vmem),
        scratch_shapes=[
            pltpu.VMEM((NF, N), jnp.int32),
            pltpu.VMEM((NF, N), jnp.int32),
            pltpu.VMEM((NF, N), jnp.int32),
            pltpu.VMEM((2, N, N), f32),
            pltpu.VMEM((2, N, N), f32),
            pltpu.VMEM((6, 2 * N, 2 * N), bf16),
            pltpu.VMEM((2 * N, NF * N), bf16),
            pltpu.VMEM((ROWS, NF * N), f32),
            pltpu.VMEM((2 * ROWS, NF * N), bf16),
            pltpu.VMEM((NOWN, 8, N), f32),
            pltpu.VMEM((NF, 8, N), f32),
            pltpu.VMEM((NF, 8, N), f32),
            pltpu.VMEM((NOWN, 8, N), f32),
            pltpu.VMEM((8 * ROWS, LANES), bf16),
            pltpu.VMEM((4 * ROWS, 2 * N), f32),
            pltpu.VMEM((N, N), f32),
            pltpu.SemaphoreType.DMA((3,)),
            pltpu.SemaphoreType.DMA((2,)),
            pltpu.SemaphoreType.DMA,
            pltpu.SemaphoreType.DMA,
            pltpu.SemaphoreType.DMA,
            pltpu.SemaphoreType.DMA((STEPS,)),
            pltpu.SemaphoreType.DMA((2,)),
        ],
        compiler_params=pltpu.CompilerParams(
            collective_id=0, has_side_effects=True, vmem_limit_bytes=40 << 20
        ),
        name="exchange",
    )(
        pltpu.with_memory_space_constraint(orbitals.reshape(2, N, N), pltpu.HBM),
        pltpu.with_memory_space_constraint(stick_cols.reshape(NF, N), pltpu.HBM),
        pltpu.with_memory_space_constraint(jnp.asarray(tables()), pltpu.HBM),
    )
    return field[None], spec[None]


def solution(mesh):
    return jax.shard_map(
        body,
        mesh=mesh,
        in_specs=(P("band", "fft", None, None), P()),
        out_specs=(P("band", "fft", None, None), P("band", None, "fft")),
        check_vma=False,
    )
```

```python
import functools
import math

import jax
import jax.numpy as jnp
import ml_dtypes
import numpy as np
from jax import lax
from jax.experimental import pallas as pl
from jax.experimental.pallas import tpu as pltpu
from jax.sharding import PartitionSpec as P

RAD = 48
N = 128
NF = 64
NBAND = 4
NOWN = 32
PER = 8
STEPS = NOWN // PER
LANES = PER * 2 * N
TILES = 5
ROWS = 8 * TILES

screening = 16.0
strength = 10.0

MESH = pl.DeviceIdType.MESH
f32 = jnp.float32
bf16 = jnp.bfloat16


def owner_device(o):
    return o // 2 * 4 + o % 2


def owner_index(f):
    return f // 4 * 2 + f % 4


def owns(f):
    return f % 4 < 2


def partner_block(o):
    return o // 2 * 4 + 3 - o % 2


def back_step(me, i):
    t = (i + 1) // 2
    return (me // 16 + t * (1 - 2 * (i % 2)) + 4) % 4


def tables():
    k = np.arange(N)
    angles = 2.0 * math.pi / N * (k[:, None] * k[None, :] % N)
    c = (np.cos(angles) + np.sin(angles)) / math.sqrt(N)

    def terms(x):
        hi = x.astype(np.float32).astype(ml_dtypes.bfloat16)
        lo = (x - hi.astype(np.float64)).astype(np.float32).astype(ml_dtypes.bfloat16)
        return hi, lo

    def left(x):
        hi, lo = terms(x)
        return np.block([[hi, hi], [lo, lo]])

    def right(x):
        hi, lo = terms(x)
        return np.block([[hi, lo], [hi, lo]])

    by_b = np.zeros((N, N))
    by_b[:, : 2 * RAD + 1] = c[:, (np.arange(2 * RAD + 1) - RAD) % N]
    by_a = np.zeros((N, N))
    for sub in range(8):
        for t in range(16):
            index = 8 * t + sub if t < 12 else 8 * (t - 4) + sub
            if sub == 7 and t >= 12:
                index = 2 * RAD if t == 15 else None
            if index is not None:
                by_a[16 * sub + t] = c[(index - RAD) % N]
    order = np.concatenate([k[0::2], k[1::2]])
    return np.stack(
        [right(by_b), left(by_a), left(c[:, order]), left(c[order]), left(by_a.T), right(by_b.T)]
    )


def two_terms(x):
    hi = x.astype(bf16)
    return hi, (x - hi.astype(f32)).astype(bf16)


def signed(x):
    return jnp.where(x < N // 2, x, x - N)


def coulomb(squared):
    kappa = squared.astype(f32)
    safe = jnp.maximum(kappa, f32(1.0))
    values = strength * screening * (1.0 - jnp.exp(-kappa / screening)) / safe
    inside = (squared > 0) & (squared <= RAD * RAD)
    return jnp.where(inside, values, f32(0.0))


def dot(a, b):
    return jnp.dot(a, b, preferred_element_type=f32)


def left_table(table, x):
    hi, lo = two_terms(x)
    both = dot(table, jnp.concatenate([hi, lo], axis=0))
    return both[:N] + both[N:]


def right_table(x, table):
    hi, lo = two_terms(x)
    both = dot(jnp.concatenate([hi, lo], axis=1), table)
    return both[:, :N] + both[:, N:]


def turn(x, groups):
    return x if groups % 4 == 0 else pltpu.roll(x, groups % 4 * 32, axis=1)


def masks():
    group = lax.broadcasted_iota(jnp.int32, (8, N), 1) // 32
    row = lax.broadcasted_iota(jnp.int32, (8, N), 0)
    return [group == i for i in range(4)], row < 4, row == 7


def by_group(groups, parts):
    low = jnp.where(groups[0], parts[0], parts[1])
    high = jnp.where(groups[2], parts[2], parts[3])
    return jnp.where(groups[0] | groups[1], low, high)


def pack(plane):
    groups, upper, last = masks()
    tiles = [[], [], [], [], []]
    for h in range(2):
        parts = [[], [], [], [], []]
        for i in range(4):
            sub = 4 * h + i
            main = plane[16 * sub : 16 * sub + 8]
            rest = plane[16 * sub + 8 : 16 * sub + 16]
            for y in range(3):
                parts[y].append(turn(main, i - y))
            second = turn(rest, i - 1)
            moved = pltpu.roll(second, 4, axis=0) if sub == 7 else second
            parts[3].append(jnp.where(upper, turn(rest, i), moved))
            third = turn(rest, i - 2)
            if sub == 0:
                third = jnp.where(upper, third, turn(main, i - 3))
            if sub == 7:
                third = jnp.where(last, second, third)
            parts[4].append(third)
        for t in range(TILES):
            tiles[t].append(by_group(groups, parts[t]))
    return [jnp.concatenate(t, axis=1) for t in tiles]


def unpack(tiles):
    groups, upper, last = masks()
    zero = jnp.zeros((8, N), f32)
    out = []
    for sub in range(8):
        h, i = sub // 4, sub % 4
        t0, t1, t2, t3, t4 = (t[:, h * N : (h + 1) * N] for t in tiles)
        special = zero
        if sub == 0:
            special = jnp.where(upper, zero, turn(t4, 3 - i))
        out.append(by_group(groups, [turn(t0, -i), turn(t1, 1 - i), turn(t2, 2 - i), special]))
        first = jnp.where(upper, turn(t3, -i), zero)
        third = jnp.where(upper, turn(t4, 2 - i), zero)
        second = turn(t3, 1 - i)
        if sub == 7:
            second = jnp.where(
                upper, pltpu.roll(second, 4, axis=0), jnp.where(last, turn(t4, 1 - i), zero)
            )
        else:
            second = jnp.where(upper, zero, second)
        out.append(by_group(groups, [first, second, third, zero]))
    return jnp.concatenate(out, axis=0)


def kernel(
    orb_hbm, cols_hbm, tab_hbm, field, spec,
    cols, places, lanes_of, own, prev, tab, pick, rowf, rowb, send1, recv1, send2, recv2, wide, acc, en,
    load_sem, orb_sem, out1_sem, in1_sem, out2_sem, in2_sem, en_sem,
):
    me = lax.axis_index("fft")
    band = lax.axis_index("band")
    is_owner = owns(me)
    mine = owner_index(me)
    before = lax.rem(band + NBAND - 1, NBAND)
    after = lax.rem(band + 1, NBAND)

    barrier = pltpu.get_barrier_semaphore()
    pl.semaphore_signal(barrier, inc=1, device_id={"band": before}, device_id_type=MESH)

    @pl.when(is_owner)
    def _():
        def greet(z, carry):
            for k in range(8):

                @pl.when(z * 8 + k != me)
                def _():
                    pl.semaphore_signal(
                        barrier, inc=1, device_id={"fft": z * 8 + k}, device_id_type=MESH
                    )

            return carry

        lax.fori_loop(0, NF // 8, greet, 0)

    loads = [
        pltpu.make_async_copy(src, dst, load_sem.at[i])
        for i, (src, dst) in enumerate(((cols_hbm, cols), (orb_hbm, own), (tab_hbm, tab)))
    ]
    y_to, x_to, z_to, z_from, x_from, y_from = (tab.at[i] for i in range(6))
    for load in loads:
        load.start()

    loads[0].wait()
    flat = cols[...]
    along_a = signed(lax.div(flat, N)) + RAD
    along_b = signed(lax.rem(flat, N)) + RAD
    inside = (along_a >= 0) & (along_a < 2 * RAD) & (along_b >= 0) & (along_b < 2 * RAD)
    big_a, big_b = along_a >> 3, along_b >> 5
    row = jnp.where(big_a < 8, 8 * big_b + big_a, 16 + 4 * big_b + big_a)
    row = jnp.where(inside, row, -1)
    lane = 32 * (along_a & 7) + (along_b & 31)
    top = (along_a == RAD) & (along_b == 2 * RAD)
    side = (along_a == 2 * RAD) & (along_b == RAD)
    places[...] = jnp.where(top, 38, jnp.where(side, 39, row))
    lanes_of[...] = jnp.where(top, 0, jnp.where(side, 240, lane))
    low_iota = lax.broadcasted_iota(jnp.int32, (2 * N, N), 0)
    row_iota = lax.broadcasted_iota(jnp.int32, (ROWS, N), 0)
    twice = lax.broadcasted_iota(jnp.int32, (2 * ROWS, N), 0)
    twice = 8 * lax.div(twice, 16) + lax.rem(twice, 8)

    def build(o):
        for blk, source in enumerate((owner_device(o), partner_block(o))):
            place = places[pl.ds(source, 1), :]
            lanes = pl.ds(pl.multiple_of((2 * o + blk) * N, N), N)
            pick[:, lanes] = jnp.where(low_iota == lanes_of[pl.ds(source, 1), :], 1.0, 0.0).astype(bf16)
            rowf[:, lanes] = jnp.where(row_iota == place, f32(1.0), f32(0.0))
            rowb[:, lanes] = jnp.where(twice == place, 1.0, 0.0).astype(bf16)

    lax.fori_loop(0, NOWN, lambda o, c: (build(o), c)[1], 0)

    @pl.when(is_owner)
    def _():
        pl.semaphore_wait(barrier, NOWN)

    @pl.when(jnp.logical_not(is_owner))
    def _():
        pl.semaphore_wait(barrier, NOWN + 1)

    give = pltpu.make_async_remote_copy(
        src_ref=own, dst_ref=prev, send_sem=orb_sem.at[0], recv_sem=orb_sem.at[1],
        device_id={"band": after}, device_id_type=MESH,
    )
    loads[1].wait()
    give.start()

    loads[2].wait()

    def forward(pair, partner, then):
        density = (own[...] * partner[...]).reshape(2 * N, N)
        along = right_table(density, y_to[...])
        planes = left_table(x_to[...], jnp.concatenate([along[:N], along[N:]], axis=1))
        packed = [pack(planes[:, :N]), pack(planes[:, N:])]
        rows = jnp.concatenate([packed[p][t] for t in range(TILES) for p in range(2)], axis=0)
        hi, lo = two_terms(rows)
        left = jnp.concatenate([hi, lo], axis=0)

        def step(i, carry):
            g = STEPS - 1 - i
            lanes = pl.ds(pl.multiple_of(g * LANES, LANES), LANES)
            picked = dot(left, pick[:, lanes])
            for plane in range(2):
                sums = None
                for t in range(TILES):
                    a = 16 * t + 8 * plane
                    both = picked[a : a + 8] + picked[2 * ROWS + a : 2 * ROWS + a + 8]
                    both = both * rowf[8 * t : 8 * t + 8, lanes]
                    sums = both if sums is None else sums + both
                total = jnp.sum(sums, axis=0, keepdims=True)
                for i in range(PER):
                    for blk in range(2):
                        at = (2 * i + blk) * N
                        row = 4 * blk + 2 * pair + plane
                        send1[PER * g + i, row : row + 1, :] = total[:, at : at + N]
            if then is not None:
                for i in range(PER):
                    then(PER * g + i)
            return carry

        lax.fori_loop(0, STEPS, step, 0)

    forward(0, own, None)

    give.wait_recv()

    def out_copy(o):
        return pltpu.make_async_remote_copy(
            src_ref=send1.at[o], dst_ref=recv1.at[me], send_sem=out1_sem, recv_sem=in1_sem,
            device_id={"fft": owner_device(o)}, device_id_type=MESH,
        )

    def send_out(o):
        @pl.when(owner_device(o) != me)
        def _():
            out_copy(o).start()

    forward(1, prev, send_out)

    @pl.when(is_owner)
    def _():
        recv1[me] = send1[mine]
        z_iota = signed(lax.broadcasted_iota(jnp.int32, (N, N), 0))
        weights = []
        for source in (me, partner_block(mine)):
            flat = cols[pl.ds(source, 1), :]
            row = signed(lax.div(flat, N))
            col = signed(lax.rem(flat, N))
            weights.append(coulomb(z_iota * z_iota + (row * row + col * col)))
        pltpu.make_async_copy(recv1.at[pl.ds(0, NF - 1)], recv1.at[pl.ds(0, NF - 1)], in1_sem).wait()
        got = recv1.reshape(NF * 8, N)
        parts = []
        for q in range(0, 8, 2):
            parts.append(
                jnp.concatenate(
                    [got[pl.ds(q, NF, stride=8), :], got[pl.ds(q + 1, NF, stride=8), :]], axis=0
                )
            )
        spectral = left_table(z_to[...], jnp.concatenate(parts, axis=1))
        v = jnp.concatenate([weights[0], weights[0], weights[1], weights[1]], axis=1)
        weighted = v * spectral
        back = left_table(z_from[...], weighted)
        put = send2.reshape(NF * 8, N)
        for q in range(8):
            a = (q % 2) * NF
            put[pl.ds(q, NF, stride=8), :] = back[a : a + NF, (q // 2) * N : (q // 2 + 1) * N]

        def send_back(z, carry):
            for k in range(8):
                peer = z * 8 + (k + 4 * (band % 2)) % 8

                @pl.when(peer != me)
                def _():
                    pltpu.make_async_remote_copy(
                        src_ref=send2.at[peer], dst_ref=recv2.at[mine], send_sem=out2_sem,
                        recv_sem=in2_sem.at[mine // PER], device_id={"fft": peer},
                        device_id_type=MESH,
                    ).start()

            return carry

        lax.fori_loop(0, NF // 8, send_back, 0)
        recv2[mine] = send2[me]
        energy = weighted * spectral
        en[...] = 0.5 * (energy[:, 2 * N : 3 * N] + energy[:, 3 * N :])
        en_copy = pltpu.make_async_remote_copy(
            src_ref=en, dst_ref=spec, send_sem=en_sem.at[0], recv_sem=en_sem.at[1],
            device_id={"fft": partner_block(mine)}, device_id_type=MESH,
        )
        en_copy.start()
        spec[...] = 0.5 * (energy[:, :N] + energy[:, N : 2 * N])

    acc[...] = jnp.zeros_like(acc)

    def gather(i, carry):
        g = back_step(me, i)
        holds_me = is_owner & (mine // PER == g)
        in_bytes = lambda n: pltpu.make_async_copy(
            recv2.at[pl.ds(0, n)], recv2.at[pl.ds(0, n)], in2_sem.at[g]
        )

        @pl.when(holds_me)
        def _():
            in_bytes(PER - 1).wait()

        @pl.when(jnp.logical_not(holds_me))
        def _():
            in_bytes(PER).wait()

        for i in range(PER):
            block = recv2[PER * g + i]
            hi = block.astype(bf16).astype(f32)
            lo = block - hi
            for blk in range(2):
                lanes = pl.ds(pl.multiple_of(g * LANES + (2 * i + blk) * N, N), N)
                at = (2 * i + blk) * N
                for term, part in enumerate((hi, lo)):
                    for r in range(0, 4, 2):
                        row = 4 * blk + r
                        two = [jnp.broadcast_to(part[q : q + 1], (8, N)) for q in (row, row + 1)]
                        one = jnp.concatenate(two, axis=0).astype(bf16)
                        for t in range(TILES):
                            a = term * 4 * ROWS + 32 * t + 8 * r
                            wide[a : a + 16, at : at + N] = rowb[16 * t : 16 * t + 16, lanes] * one
        lanes = pl.ds(pl.multiple_of(g * LANES, LANES), LANES)
        both = lax.dot_general(
            wide[...], pick[:, lanes], (((1,), (1,)), ((), ())), preferred_element_type=f32
        )
        acc[...] += both[: 4 * ROWS] + both[4 * ROWS :]
        return carry

    lax.fori_loop(0, STEPS, gather, 0)

    freq = jnp.concatenate(
        [unpack([acc[32 * t + 8 * r : 32 * t + 8 * r + 8, :] for t in range(TILES)]) for r in range(4)],
        axis=1,
    )
    rows = left_table(x_from[...], freq)
    pot = right_table(
        jnp.concatenate([rows[:, r * N : (r + 1) * N] for r in range(4)], axis=0), y_from[...]
    )
    total = pot[: 2 * N] * own[...].reshape(2 * N, N) + pot[2 * N :] * prev[...].reshape(2 * N, N)
    field[...] = (-total).reshape(2, N, N)

    give.wait_send()

    def sent(n, buf, sem):
        pltpu.make_async_copy(buf.at[pl.ds(0, n)], buf.at[pl.ds(0, n)], sem).wait()

    @pl.when(is_owner)
    def _():
        sent(NOWN - 1, send1, out1_sem)
        sent(NF - 1, send2, out2_sem)
        pltpu.make_async_copy(en, en, en_sem.at[0]).wait()

    @pl.when(jnp.logical_not(is_owner))
    def _():
        sent(NOWN, send1, out1_sem)
        pltpu.make_async_copy(en, en, en_sem.at[1]).wait()


def body(orbitals, stick_cols):
    anywhere = pl.BlockSpec(memory_space=pltpu.HBM)
    vmem = pl.BlockSpec(memory_space=pltpu.VMEM)
    field, spec = pl.pallas_call(
        kernel,
        out_shape=(
            jax.ShapeDtypeStruct((2, N, N), f32),
            jax.ShapeDtypeStruct((N, N), f32),
        ),
        in_specs=[anywhere] * 3,
        out_specs=(vmem, vmem),
        scratch_shapes=[
            pltpu.VMEM((NF, N), jnp.int32),
            pltpu.VMEM((NF, N), jnp.int32),
            pltpu.VMEM((NF, N), jnp.int32),
            pltpu.VMEM((2, N, N), f32),
            pltpu.VMEM((2, N, N), f32),
            pltpu.VMEM((6, 2 * N, 2 * N), bf16),
            pltpu.VMEM((2 * N, NF * N), bf16),
            pltpu.VMEM((ROWS, NF * N), f32),
            pltpu.VMEM((2 * ROWS, NF * N), bf16),
            pltpu.VMEM((NOWN, 8, N), f32),
            pltpu.VMEM((NF, 8, N), f32),
            pltpu.VMEM((NF, 8, N), f32),
            pltpu.VMEM((NOWN, 8, N), f32),
            pltpu.VMEM((8 * ROWS, LANES), bf16),
            pltpu.VMEM((4 * ROWS, 2 * N), f32),
            pltpu.VMEM((N, N), f32),
            pltpu.SemaphoreType.DMA((3,)),
            pltpu.SemaphoreType.DMA((2,)),
            pltpu.SemaphoreType.DMA,
            pltpu.SemaphoreType.DMA,
            pltpu.SemaphoreType.DMA,
            pltpu.SemaphoreType.DMA((STEPS,)),
            pltpu.SemaphoreType.DMA((2,)),
        ],
        compiler_params=pltpu.CompilerParams(
            collective_id=0, has_side_effects=True, vmem_limit_bytes=40 << 20
        ),
        name="exchange",
    )(
        pltpu.with_memory_space_constraint(orbitals.reshape(2, N, N), pltpu.HBM),
        pltpu.with_memory_space_constraint(stick_cols.reshape(NF, N), pltpu.HBM),
        pltpu.with_memory_space_constraint(jnp.asarray(tables()), pltpu.HBM),
    )
    return field[None], spec[None]


def solution(mesh):
    return jax.shard_map(
        body,
        mesh=mesh,
        in_specs=(P("band", "fft", None, None), P()),
        out_specs=(P("band", "fft", None, None), P("band", None, "fft")),
        check_vma=False,
    )
```

```python
import functools
import math

import jax
import jax.numpy as jnp
import ml_dtypes
import numpy as np
from jax import lax
from jax.experimental import pallas as pl
from jax.experimental.pallas import tpu as pltpu
from jax.sharding import PartitionSpec as P

RAD = 48
N = 128
NF = 64
NBAND = 4
NOWN = 32
PER = 8
STEPS = NOWN // PER
LANES = PER * 2 * N
TILES = 5
ROWS = 8 * TILES

screening = 16.0
strength = 10.0

MESH = pl.DeviceIdType.MESH
f32 = jnp.float32
bf16 = jnp.bfloat16


def owner_device(o):
    return o // 2 * 4 + o % 2


def owner_index(f):
    return f // 4 * 2 + f % 4


def owns(f):
    return f % 4 < 2


def partner_block(o):
    return o // 2 * 4 + 3 - o % 2


def back_step(me, i):
    t = (i + 1) // 2
    return (me // 16 + t * (1 - 2 * (i % 2)) + 4) % 4


def tables():
    k = np.arange(N)
    angles = 2.0 * math.pi / N * (k[:, None] * k[None, :] % N)
    c = (np.cos(angles) + np.sin(angles)) / math.sqrt(N)

    def terms(x):
        hi = x.astype(np.float32).astype(ml_dtypes.bfloat16)
        lo = (x - hi.astype(np.float64)).astype(np.float32).astype(ml_dtypes.bfloat16)
        return hi, lo

    def left(x):
        hi, lo = terms(x)
        return np.block([[hi, hi], [lo, lo]])

    def right(x):
        hi, lo = terms(x)
        return np.block([[hi, lo], [hi, lo]])

    by_b = np.zeros((N, N))
    by_b[:, : 2 * RAD + 1] = c[:, (np.arange(2 * RAD + 1) - RAD) % N]
    by_a = np.zeros((N, N))
    for sub in range(8):
        for t in range(16):
            index = 8 * t + sub if t < 12 else 8 * (t - 4) + sub
            if sub == 7 and t >= 12:
                index = 2 * RAD if t == 15 else None
            if index is not None:
                by_a[16 * sub + t] = c[(index - RAD) % N]
    order = np.concatenate([k[0::2], k[1::2]])
    return np.stack(
        [right(by_b), left(by_a), left(c[:, order]), left(c[order]), left(by_a.T), right(by_b.T)]
    )


def two_terms(x):
    hi = x.astype(bf16)
    return hi, (x - hi.astype(f32)).astype(bf16)


def signed(x):
    return jnp.where(x < N // 2, x, x - N)


def coulomb(squared):
    kappa = squared.astype(f32)
    safe = jnp.maximum(kappa, f32(1.0))
    values = strength * screening * (1.0 - jnp.exp(-kappa / screening)) / safe
    inside = (squared > 0) & (squared <= RAD * RAD)
    return jnp.where(inside, values, f32(0.0))


def dot(a, b):
    return jnp.dot(a, b, preferred_element_type=f32)


def left_table(table, x):
    hi, lo = two_terms(x)
    both = dot(table, jnp.concatenate([hi, lo], axis=0))
    return both[:N] + both[N:]


def right_table(x, table):
    hi, lo = two_terms(x)
    both = dot(jnp.concatenate([hi, lo], axis=1), table)
    return both[:, :N] + both[:, N:]


def turn(x, groups):
    return x if groups % 4 == 0 else pltpu.roll(x, groups % 4 * 32, axis=1)


def masks():
    group = lax.broadcasted_iota(jnp.int32, (8, N), 1) // 32
    row = lax.broadcasted_iota(jnp.int32, (8, N), 0)
    return [group == i for i in range(4)], row < 4, row == 7


def by_group(groups, parts):
    low = jnp.where(groups[0], parts[0], parts[1])
    high = jnp.where(groups[2], parts[2], parts[3])
    return jnp.where(groups[0] | groups[1], low, high)


def pack(plane):
    groups, upper, last = masks()
    tiles = [[], [], [], [], []]
    for h in range(2):
        parts = [[], [], [], [], []]
        for i in range(4):
            sub = 4 * h + i
            main = plane[16 * sub : 16 * sub + 8]
            rest = plane[16 * sub + 8 : 16 * sub + 16]
            for y in range(3):
                parts[y].append(turn(main, i - y))
            second = turn(rest, i - 1)
            moved = pltpu.roll(second, 4, axis=0) if sub == 7 else second
            parts[3].append(jnp.where(upper, turn(rest, i), moved))
            third = turn(rest, i - 2)
            if sub == 0:
                third = jnp.where(upper, third, turn(main, i - 3))
            if sub == 7:
                third = jnp.where(last, second, third)
            parts[4].append(third)
        for t in range(TILES):
            tiles[t].append(by_group(groups, parts[t]))
    return [jnp.concatenate(t, axis=1) for t in tiles]


def unpack(tiles):
    groups, upper, last = masks()
    zero = jnp.zeros((8, N), f32)
    out = []
    for sub in range(8):
        h, i = sub // 4, sub % 4
        t0, t1, t2, t3, t4 = (t[:, h * N : (h + 1) * N] for t in tiles)
        special = zero
        if sub == 0:
            special = jnp.where(upper, zero, turn(t4, 3 - i))
        out.append(by_group(groups, [turn(t0, -i), turn(t1, 1 - i), turn(t2, 2 - i), special]))
        first = jnp.where(upper, turn(t3, -i), zero)
        third = jnp.where(upper, turn(t4, 2 - i), zero)
        second = turn(t3, 1 - i)
        if sub == 7:
            second = jnp.where(
                upper, pltpu.roll(second, 4, axis=0), jnp.where(last, turn(t4, 1 - i), zero)
            )
        else:
            second = jnp.where(upper, zero, second)
        out.append(by_group(groups, [first, second, third, zero]))
    return jnp.concatenate(out, axis=0)


def kernel(
    orb_hbm, cols_hbm, tab_hbm, field, spec,
    cols, places, lanes_of, own, prev, tab, pick, rowf, rowb, send1, recv1, send2, recv2, wide, acc, en,
    load_sem, orb_sem, out1_sem, in1_sem, out2_sem, in2_sem, en_sem,
):
    me = lax.axis_index("fft")
    band = lax.axis_index("band")
    is_owner = owns(me)
    mine = owner_index(me)
    before = lax.rem(band + NBAND - 1, NBAND)
    after = lax.rem(band + 1, NBAND)

    barrier = pltpu.get_barrier_semaphore()
    pl.semaphore_signal(barrier, inc=1, device_id={"band": before}, device_id_type=MESH)

    @pl.when(is_owner)
    def _():
        def greet(z, carry):
            for k in range(8):

                @pl.when(z * 8 + k != me)
                def _():
                    pl.semaphore_signal(
                        barrier, inc=1, device_id={"fft": z * 8 + k}, device_id_type=MESH
                    )

            return carry

        lax.fori_loop(0, NF // 8, greet, 0)

    loads = [
        pltpu.make_async_copy(src, dst, load_sem.at[i])
        for i, (src, dst) in enumerate(((cols_hbm, cols), (orb_hbm, own), (tab_hbm, tab)))
    ]
    y_to, x_to, z_to, z_from, x_from, y_from = (tab.at[i] for i in range(6))
    for load in loads:
        load.start()

    loads[0].wait()
    flat = cols[...]
    along_a = signed(lax.div(flat, N)) + RAD
    along_b = signed(lax.rem(flat, N)) + RAD
    inside = (along_a >= 0) & (along_a < 2 * RAD) & (along_b >= 0) & (along_b < 2 * RAD)
    big_a, big_b = along_a >> 3, along_b >> 5
    row = jnp.where(big_a < 8, 8 * big_b + big_a, 16 + 4 * big_b + big_a)
    row = jnp.where(inside, row, -1)
    lane = 32 * (along_a & 7) + (along_b & 31)
    top = (along_a == RAD) & (along_b == 2 * RAD)
    side = (along_a == 2 * RAD) & (along_b == RAD)
    places[...] = jnp.where(top, 38, jnp.where(side, 39, row))
    lanes_of[...] = jnp.where(top, 0, jnp.where(side, 240, lane))
    low_iota = lax.broadcasted_iota(jnp.int32, (2 * N, N), 0)
    row_iota = lax.broadcasted_iota(jnp.int32, (ROWS, N), 0)
    twice = lax.broadcasted_iota(jnp.int32, (2 * ROWS, N), 0)
    twice = 8 * lax.div(twice, 16) + lax.rem(twice, 8)

    def build(o):
        for blk, source in enumerate((owner_device(o), partner_block(o))):
            place = places[pl.ds(source, 1), :]
            lanes = pl.ds(pl.multiple_of((2 * o + blk) * N, N), N)
            pick[:, lanes] = jnp.where(low_iota == lanes_of[pl.ds(source, 1), :], 1.0, 0.0).astype(bf16)
            rowf[:, lanes] = jnp.where(row_iota == place, f32(1.0), f32(0.0))
            rowb[:, lanes] = jnp.where(twice == place, 1.0, 0.0).astype(bf16)

    lax.fori_loop(0, NOWN, lambda o, c: (build(o), c)[1], 0)

    loads[1].wait()
    loads[2].wait()

    def forward(pair, partner, then):
        density = (own[...] * partner[...]).reshape(2 * N, N)
        along = right_table(density, y_to[...])
        planes = left_table(x_to[...], jnp.concatenate([along[:N], along[N:]], axis=1))
        packed = [pack(planes[:, :N]), pack(planes[:, N:])]
        rows = jnp.concatenate([packed[p][t] for t in range(TILES) for p in range(2)], axis=0)
        hi, lo = two_terms(rows)
        left = jnp.concatenate([hi, lo], axis=0)

        def step(i, carry):
            g = STEPS - 1 - i
            lanes = pl.ds(pl.multiple_of(g * LANES, LANES), LANES)
            picked = dot(left, pick[:, lanes])
            for plane in range(2):
                sums = None
                for t in range(TILES):
                    a = 16 * t + 8 * plane
                    both = picked[a : a + 8] + picked[2 * ROWS + a : 2 * ROWS + a + 8]
                    both = both * rowf[8 * t : 8 * t + 8, lanes]
                    sums = both if sums is None else sums + both
                total = jnp.sum(sums, axis=0, keepdims=True)
                for i in range(PER):
                    for blk in range(2):
                        at = (2 * i + blk) * N
                        row = 4 * blk + 2 * pair + plane
                        send1[PER * g + i, row : row + 1, :] = total[:, at : at + N]
            if then is not None:
                for i in range(PER):
                    then(PER * g + i)
            return carry

        lax.fori_loop(0, STEPS, step, 0)

    forward(0, own, None)

    @pl.when(is_owner)
    def _():
        pl.semaphore_wait(barrier, NOWN)

    @pl.when(jnp.logical_not(is_owner))
    def _():
        pl.semaphore_wait(barrier, NOWN + 1)

    give = pltpu.make_async_remote_copy(
        src_ref=own, dst_ref=prev, send_sem=orb_sem.at[0], recv_sem=orb_sem.at[1],
        device_id={"band": after}, device_id_type=MESH,
    )
    give.start()


    give.wait_recv()

    def out_copy(o):
        return pltpu.make_async_remote_copy(
            src_ref=send1.at[o], dst_ref=recv1.at[me], send_sem=out1_sem, recv_sem=in1_sem,
            device_id={"fft": owner_device(o)}, device_id_type=MESH,
        )

    def send_out(o):
        @pl.when(owner_device(o) != me)
        def _():
            out_copy(o).start()

    forward(1, prev, send_out)

    @pl.when(is_owner)
    def _():
        recv1[me] = send1[mine]
        z_iota = signed(lax.broadcasted_iota(jnp.int32, (N, N), 0))
        weights = []
        for source in (me, partner_block(mine)):
            flat = cols[pl.ds(source, 1), :]
            row = signed(lax.div(flat, N))
            col = signed(lax.rem(flat, N))
            weights.append(coulomb(z_iota * z_iota + (row * row + col * col)))
        pltpu.make_async_copy(recv1.at[pl.ds(0, NF - 1)], recv1.at[pl.ds(0, NF - 1)], in1_sem).wait()
        got = recv1.reshape(NF * 8, N)
        parts = []
        for q in range(0, 8, 2):
            parts.append(
                jnp.concatenate(
                    [got[pl.ds(q, NF, stride=8), :], got[pl.ds(q + 1, NF, stride=8), :]], axis=0
                )
            )
        spectral = left_table(z_to[...], jnp.concatenate(parts, axis=1))
        v = jnp.concatenate([weights[0], weights[0], weights[1], weights[1]], axis=1)
        weighted = v * spectral
        back = left_table(z_from[...], weighted)
        put = send2.reshape(NF * 8, N)
        for q in range(8):
            a = (q % 2) * NF
            put[pl.ds(q, NF, stride=8), :] = back[a : a + NF, (q // 2) * N : (q // 2 + 1) * N]

        def send_back(z, carry):
            for k in range(8):
                peer = z * 8 + (k + 4 * (band % 2)) % 8

                @pl.when(peer != me)
                def _():
                    pltpu.make_async_remote_copy(
                        src_ref=send2.at[peer], dst_ref=recv2.at[mine], send_sem=out2_sem,
                        recv_sem=in2_sem.at[mine // PER], device_id={"fft": peer},
                        device_id_type=MESH,
                    ).start()

            return carry

        lax.fori_loop(0, NF // 8, send_back, 0)
        recv2[mine] = send2[me]
        energy = weighted * spectral
        en[...] = 0.5 * (energy[:, 2 * N : 3 * N] + energy[:, 3 * N :])
        en_copy = pltpu.make_async_remote_copy(
            src_ref=en, dst_ref=spec, send_sem=en_sem.at[0], recv_sem=en_sem.at[1],
            device_id={"fft": partner_block(mine)}, device_id_type=MESH,
        )
        en_copy.start()
        spec[...] = 0.5 * (energy[:, :N] + energy[:, N : 2 * N])

    acc[...] = jnp.zeros_like(acc)

    def gather(i, carry):
        g = back_step(me, i)
        holds_me = is_owner & (mine // PER == g)
        in_bytes = lambda n: pltpu.make_async_copy(
            recv2.at[pl.ds(0, n)], recv2.at[pl.ds(0, n)], in2_sem.at[g]
        )

        @pl.when(holds_me)
        def _():
            in_bytes(PER - 1).wait()

        @pl.when(jnp.logical_not(holds_me))
        def _():
            in_bytes(PER).wait()

        for i in range(PER):
            block = recv2[PER * g + i]
            hi = block.astype(bf16).astype(f32)
            lo = block - hi
            for blk in range(2):
                lanes = pl.ds(pl.multiple_of(g * LANES + (2 * i + blk) * N, N), N)
                at = (2 * i + blk) * N
                for term, part in enumerate((hi, lo)):
                    for r in range(0, 4, 2):
                        row = 4 * blk + r
                        two = [jnp.broadcast_to(part[q : q + 1], (8, N)) for q in (row, row + 1)]
                        one = jnp.concatenate(two, axis=0).astype(bf16)
                        for t in range(TILES):
                            a = term * 4 * ROWS + 32 * t + 8 * r
                            wide[a : a + 16, at : at + N] = rowb[16 * t : 16 * t + 16, lanes] * one
        lanes = pl.ds(pl.multiple_of(g * LANES, LANES), LANES)
        both = lax.dot_general(
            wide[...], pick[:, lanes], (((1,), (1,)), ((), ())), preferred_element_type=f32
        )
        acc[...] += both[: 4 * ROWS] + both[4 * ROWS :]
        return carry

    lax.fori_loop(0, STEPS, gather, 0)

    freq = jnp.concatenate(
        [unpack([acc[32 * t + 8 * r : 32 * t + 8 * r + 8, :] for t in range(TILES)]) for r in range(4)],
        axis=1,
    )
    rows = left_table(x_from[...], freq)
    pot = right_table(
        jnp.concatenate([rows[:, r * N : (r + 1) * N] for r in range(4)], axis=0), y_from[...]
    )
    total = pot[: 2 * N] * own[...].reshape(2 * N, N) + pot[2 * N :] * prev[...].reshape(2 * N, N)
    field[...] = (-total).reshape(2, N, N)

    give.wait_send()

    def sent(n, buf, sem):
        pltpu.make_async_copy(buf.at[pl.ds(0, n)], buf.at[pl.ds(0, n)], sem).wait()

    @pl.when(is_owner)
    def _():
        sent(NOWN - 1, send1, out1_sem)
        sent(NF - 1, send2, out2_sem)
        pltpu.make_async_copy(en, en, en_sem.at[0]).wait()

    @pl.when(jnp.logical_not(is_owner))
    def _():
        sent(NOWN, send1, out1_sem)
        pltpu.make_async_copy(en, en, en_sem.at[1]).wait()


def body(orbitals, stick_cols):
    anywhere = pl.BlockSpec(memory_space=pltpu.HBM)
    vmem = pl.BlockSpec(memory_space=pltpu.VMEM)
    field, spec = pl.pallas_call(
        kernel,
        out_shape=(
            jax.ShapeDtypeStruct((2, N, N), f32),
            jax.ShapeDtypeStruct((N, N), f32),
        ),
        in_specs=[anywhere] * 3,
        out_specs=(vmem, vmem),
        scratch_shapes=[
            pltpu.VMEM((NF, N), jnp.int32),
            pltpu.VMEM((NF, N), jnp.int32),
            pltpu.VMEM((NF, N), jnp.int32),
            pltpu.VMEM((2, N, N), f32),
            pltpu.VMEM((2, N, N), f32),
            pltpu.VMEM((6, 2 * N, 2 * N), bf16),
            pltpu.VMEM((2 * N, NF * N), bf16),
            pltpu.VMEM((ROWS, NF * N), f32),
            pltpu.VMEM((2 * ROWS, NF * N), bf16),
            pltpu.VMEM((NOWN, 8, N), f32),
            pltpu.VMEM((NF, 8, N), f32),
            pltpu.VMEM((NF, 8, N), f32),
            pltpu.VMEM((NOWN, 8, N), f32),
            pltpu.VMEM((8 * ROWS, LANES), bf16),
            pltpu.VMEM((4 * ROWS, 2 * N), f32),
            pltpu.VMEM((N, N), f32),
            pltpu.SemaphoreType.DMA((3,)),
            pltpu.SemaphoreType.DMA((2,)),
            pltpu.SemaphoreType.DMA,
            pltpu.SemaphoreType.DMA,
            pltpu.SemaphoreType.DMA,
            pltpu.SemaphoreType.DMA((STEPS,)),
            pltpu.SemaphoreType.DMA((2,)),
        ],
        compiler_params=pltpu.CompilerParams(
            collective_id=0, has_side_effects=True, vmem_limit_bytes=40 << 20
        ),
        name="exchange",
    )(
        pltpu.with_memory_space_constraint(orbitals.reshape(2, N, N), pltpu.HBM),
        pltpu.with_memory_space_constraint(stick_cols.reshape(NF, N), pltpu.HBM),
        pltpu.with_memory_space_constraint(jnp.asarray(tables()), pltpu.HBM),
    )
    return field[None], spec[None]


def solution(mesh):
    return jax.shard_map(
        body,
        mesh=mesh,
        in_specs=(P("band", "fft", None, None), P()),
        out_specs=(P("band", "fft", None, None), P("band", None, "fft")),
        check_vma=False,
    )
```
